32 devices in a mesh: streams: 8 (over z, y), mp: 4 (over x, core).
Axes of the slice: x: 2, y: 2, z: 4, core: 2. Of those that a mesh axis runs over, the one named last changes fastest.
Arguments:
- frames: bfloat16 [3072, 1536], P('streams', 'mp'), may hold values from -6 to 6
- convolution_cache: bfloat16 [256, 31, 1536], P('streams', None, 'mp'), may hold values from -6 to 6
- destination: int32 [256], P('streams'), may hold values from 0 to 7, as said below
- tenant: int32 [256], P('streams'), may hold values from 0 to 3
- valid: int32 [256], P('streams'), may hold values from 1 to 4
- tenant_panel_slot: int32 [4], replicated, may hold values from 0 to 7, as said below
- input_weight: bfloat16 [1536, 2, 1536], P(None, None, 'mp'), may hold values from -0.15625 to 0.15625
- tenant_down_weight: bfloat16 [8, 1536, 16], P('streams', 'mp'), may hold values from -0.15625 to 0.15625
- tenant_up_weight: bfloat16 [8, 16, 2, 1536], P('streams', None, None, 'mp'), may hold values from -1.5 to 1.5
- depthwise_taps: float32 [32, 1536], P(None, 'mp'), may hold values from -1 to 1
- batchnorm_scale: float32 [1536], P('mp'), may hold values from 0.25 to 1.75
- batchnorm_offset: float32 [1536], P('mp'), may hold values from -3 to 3
Outputs:
- encoded: bfloat16 [3072, 1536], P('streams', 'mp')
The draws below stay inside these ranges and needn't reach their ends.
Inputs may be any that keep to these rules, and one draw needn't show every extreme that they name: `destination`: for every slot index below 32, the streams in that slot of all devices go to distinct devices, so every device receives exactly one stream in each slot. One device sends exactly 4 streams to each device that it sends to. `tenant_panel_slot`: distinct slots.
All inputs are finite; a program needn't handle non-finite values.
Results may differ from the reference program's by a relative error of at most 0.0027.
Values may be sent and summed in bfloat16 or wider, within the bound.
A program may use at most 128 MiB of HBM per device.

```python
import math
import jax
import jax.numpy as jnp
import numpy as np
from jax import lax

MODEL_WIDTH = 1536
KC = 32
ADAPTER_RANK = 16
NCH = 4
CH = 3
STREAMS_PER_SHARD = 32
FR = 12
STREAMS = 256
ROWS = 3072
NT = 4
N_STREAMS = 8


def draw_destination(key, part):
    per_peer = max(1, STREAMS_PER_SHARD // N_STREAMS)
    groups = STREAMS_PER_SHARD // per_peer
    first_key, second_key = jax.random.split(jax.random.fold_in(key, 11))
    shuffle = jax.random.permutation(first_key, N_STREAMS)
    inverse = jnp.argsort(shuffle)
    shifts = jax.random.permutation(second_key, N_STREAMS)[:groups]
    stream_index = jnp.arange(STREAMS_PER_SHARD * N_STREAMS, dtype=jnp.int32)
    owner = stream_index // STREAMS_PER_SHARD
    slot_index = stream_index % STREAMS_PER_SHARD
    return shuffle[(inverse[owner] + shifts[slot_index // per_peer]) % N_STREAMS].astype(jnp.int32)


def draw_tenant_panel_slot(key, part):
    first_key, second_key = jax.random.split(jax.random.fold_in(key, 23))
    others = jax.random.permutation(first_key, N_STREAMS - 1)[:NT - 1].astype(jnp.int32)
    values = jnp.concatenate([others, jnp.full((1,), N_STREAMS - 1, dtype=jnp.int32)])
    order = jax.random.permutation(second_key, NT)
    return values[order].astype(jnp.int32)


def with_ends(result, key, low, largest):
    longest = result.shape.index(max(result.shape))
    spots = []
    for shift in (0, 1):
        where = [jax.random.randint(jax.random.fold_in(key, axis), (), 0, length) for axis, length in enumerate(result.shape)]
        where[longest] = (where[longest] + shift) % result.shape[longest]
        spots.append(tuple(where))
    return result.at[spots[0]].set(low).at[spots[1]].set(largest)


def block_levels(key, dims, cuts, smallest, largest):
    def one(axis_at, parts):
        steps = jax.random.uniform(jax.random.fold_in(jax.random.fold_in(key, 6), axis_at), (parts,), jnp.float32, smallest / len(cuts), largest / len(cuts))
        return jnp.repeat(jnp.exp(steps), dims[axis_at] // parts).reshape((-1,) + (1,) * (len(dims) - axis_at - 1))

    loudness = one(*cuts[0])
    for cut in cuts[1:]:
        loudness = loudness * one(*cut)
    return loudness


def rank_bounds(count, skew):
    weights = [(1 << 20) // math.isqrt(grade ** skew) + 1 for grade in range(1, count + 1)]
    width = 1 + sum(weights) // (1 << 30)
    return np.cumsum(np.array([max(1, weight // width) for weight in weights]))


def skewed_ids(key, shape, amount, slope):
    grid = rank_bounds(amount, slope)
    lot = jax.random.randint(jax.random.fold_in(key, 1), shape, 0, int(grid[amount - 1]))
    standing = jnp.searchsorted(jnp.asarray(grid, jnp.int32), lot, side="right")
    return jax.random.permutation(jax.random.fold_in(key, 2), amount)[standing].astype(jnp.int32)


def bell_draw(own_key, extent, spread, limit, pieces=(), kind=jnp.bfloat16):
    factor_of = block_levels(own_key, extent, pieces, -0.22, 0.18) if pieces else 1.0
    drawn = jax.random.normal(own_key, extent, jnp.float32) * spread * factor_of
    return jnp.minimum(jnp.maximum(drawn, -limit), limit).astype(kind)


def setup_inputs(seed: int = 0) -> dict:
    arg_keys = jax.random.split(jax.random.key(seed), 13)
    frames = bell_draw(arg_keys[0], (ROWS, MODEL_WIDTH), 1.0, 6.0, ((0, 8), (1, 4)))
    convolution_cache = bell_draw(arg_keys[1], (STREAMS, KC - 1, MODEL_WIDTH), 1.0, 6.0, ((0, 8), (2, 4)))
    destination = draw_destination(jax.random.fold_in(arg_keys[12], 71), 0)
    tenant = with_ends(skewed_ids(arg_keys[3], (STREAMS,), NT, 2), jax.random.fold_in(arg_keys[3], 3), 0, NT - 1).astype(jnp.int32)
    valid = with_ends(jax.random.randint(arg_keys[4], (STREAMS,), 1, NCH + 1), jax.random.fold_in(arg_keys[4], 1), 1, NCH).astype(jnp.int32)
    tenant_panel_slot = draw_tenant_panel_slot(jax.random.fold_in(arg_keys[12], 71), 0)
    input_weight = bell_draw(arg_keys[6], (MODEL_WIDTH, 2, MODEL_WIDTH), MODEL_WIDTH ** -0.5, 0.15625, ((2, 4),))
    tenant_down_weight = bell_draw(arg_keys[7], (N_STREAMS, MODEL_WIDTH, ADAPTER_RANK), MODEL_WIDTH ** -0.5, 0.15625, ((0, 8), (1, 4)))
    tenant_up_weight = bell_draw(arg_keys[8], (N_STREAMS, ADAPTER_RANK, 2, MODEL_WIDTH), ADAPTER_RANK ** -0.5, 1.5, ((0, 8), (3, 4)))
    depthwise_taps = bell_draw(arg_keys[9], (KC, MODEL_WIDTH), KC ** -0.5, 1.0, ((1, 4),), jnp.float32)
    batchnorm_scale = jnp.clip(1.0 + 0.15 * jax.random.normal(arg_keys[10], (MODEL_WIDTH,), jnp.float32), 0.25, 1.75)
    batchnorm_offset = bell_draw(arg_keys[11], (MODEL_WIDTH,), 0.5, 3.0, ((0, 4),), jnp.float32)
    return dict(frames=frames, convolution_cache=convolution_cache, destination=destination, tenant=tenant, valid=valid, tenant_panel_slot=tenant_panel_slot, input_weight=input_weight, tenant_down_weight=tenant_down_weight, tenant_up_weight=tenant_up_weight, depthwise_taps=depthwise_taps, batchnorm_scale=batchnorm_scale, batchnorm_offset=batchnorm_offset)


def reference(frames, convolution_cache, destination, tenant, valid, tenant_panel_slot, input_weight, tenant_down_weight, tenant_up_weight, depthwise_taps, batchnorm_scale, batchnorm_offset):
    old_index = jnp.arange(STREAMS, dtype=jnp.int32)
    new_index = (destination.astype(jnp.int32) * STREAMS_PER_SHARD + old_index % STREAMS_PER_SHARD).astype(jnp.int32)
    moved = jnp.zeros_like(convolution_cache).at[new_index].set(convolution_cache)
    stream_slot = tenant_panel_slot[tenant].astype(jnp.int32)
    w_flat = input_weight.reshape(MODEL_WIDTH, 2 * MODEL_WIDTH)
    blocks = (frames.reshape(N_STREAMS, STREAMS_PER_SHARD * FR, MODEL_WIDTH), moved.reshape(N_STREAMS, STREAMS_PER_SHARD, KC - 1, MODEL_WIDTH),
              stream_slot.reshape(N_STREAMS, STREAMS_PER_SHARD), valid.reshape(N_STREAMS, STREAMS_PER_SHARD))

    def run_block(item):
        block_rows, block_cache, block_panel_slot, block_valid = item
        base = jnp.dot(block_rows, w_flat, preferred_element_type=jnp.float32)
        down_result = tenant_down_weight[block_panel_slot].astype(jnp.float32)
        upper_result = tenant_up_weight[block_panel_slot].reshape(STREAMS_PER_SHARD, ADAPTER_RANK, 2 * MODEL_WIDTH).astype(jnp.float32)
        grouped = block_rows.reshape(STREAMS_PER_SHARD, FR, MODEL_WIDTH).astype(jnp.float32)
        low = jnp.einsum("sfd,sdk->sfk", grouped, down_result).astype(jnp.bfloat16)
        lift = jnp.einsum("sfk,skc->sfc", low.astype(jnp.float32), upper_result)
        pre = base.reshape(STREAMS_PER_SHARD, FR, 2 * MODEL_WIDTH) + lift
        gated = (pre[:, :, :MODEL_WIDTH] * jax.nn.sigmoid(pre[:, :, MODEL_WIDTH:])).astype(jnp.bfloat16)
        sequence = jnp.concatenate([block_cache, gated], axis=1)
        mixed = jnp.zeros((STREAMS_PER_SHARD, FR, MODEL_WIDTH), jnp.float32)
        for tap_index in range(KC):
            mixed = mixed + sequence[:, tap_index:tap_index + FR, :].astype(jnp.float32) * depthwise_taps[tap_index][None, None, :]
        normed = mixed * batchnorm_scale + batchnorm_offset
        active = normed * jax.nn.sigmoid(normed)
        frame_index = jnp.arange(FR, dtype=jnp.int32)
        keep = frame_index[None, :] < (block_valid.astype(jnp.int32) * CH)[:, None]
        return jnp.where(keep[:, :, None], active, jnp.zeros_like(active)).astype(jnp.bfloat16)

    encoded = lax.map(run_block, blocks)
    return encoded.reshape(ROWS, MODEL_WIDTH)
```

```python
import functools

import jax
import jax.numpy as jnp
from jax import lax
from jax.experimental import pallas as pl
from jax.experimental.pallas import tpu as pltpu
from jax.sharding import PartitionSpec as P

CH = 3
MESH = pl.DeviceIdType.MESH
F32 = jnp.float32
BF16 = jnp.bfloat16


def iota(shape, dim):
    return lax.broadcasted_iota(jnp.int32, shape, dim)


def kernel(
    dims,
    pick_s, tenant_s, valid_s, panel_s,
    frames, cache, dest, weight_hbm, down, up, taps, scale, offset,
    out,
    gathered, outgoing, arrived, destall, downg, upg, lows, weight, acc, seq, enc,
    w_sem, f_send, f_recv, c_send, c_recv, d_send, d_recv, a_send, a_recv, u_send, u_recv,
    l_send, l_recv,
):
    peers, mps, count, fr, hist, width, per_peer, rank_dim = dims
    rows = count * fr
    me = lax.axis_index("streams")
    my = lax.axis_index("mp")

    w_copy = pltpu.make_async_copy(weight_hbm, weight, w_sem)
    w_copy.start()

    barrier = pltpu.get_barrier_semaphore()
    for o in range(1, mps):
        pl.semaphore_signal(
            barrier, inc=1, device_id={"mp": lax.rem(my + o, mps)}, device_id_type=MESH
        )

    def greet(o, c):
        pl.semaphore_signal(
            barrier, inc=1, device_id={"streams": lax.rem(me + o, peers)}, device_id_type=MESH
        )
        return c

    lax.fori_loop(1, peers, greet, 0)

    r_i, c_i = iota((rows, rows), 0), iota((rows, rows), 1)
    perm = jnp.where(c_i == (r_i % count) * fr + r_i // count, 1.0, 0.0).astype(BF16)
    mine = jnp.dot(perm, frames[...], preferred_element_type=F32).astype(BF16)
    gathered[my] = mine

    outgoing[:, hist:, :] = jnp.zeros((peers * per_peer, outgoing.shape[1] - hist, width), BF16)

    def pack(b, c):
        outgoing[b, :hist, :] = cache[pick_s[b]]
        return c

    lax.fori_loop(0, peers * per_peer, pack, 0)

    pl.semaphore_wait(barrier, peers - 1 + mps - 1)

    def remote(src, dst, send, recv, where):
        return pltpu.make_async_remote_copy(
            src_ref=src, dst_ref=dst, send_sem=send, recv_sem=recv,
            device_id=where, device_id_type=MESH,
        )

    def down_copy(o):
        to = {"streams": lax.rem(me + o, peers)}
        return remote(down, downg.at[me], a_send.at[o], a_recv.at[o], to)

    def up_copy(o):
        to = {"streams": lax.rem(me + o, peers)}
        return remote(up, upg.at[me], u_send.at[o], u_recv.at[o], to)

    def dest_copy(o):
        to = {"streams": lax.rem(me + o, peers)}
        return remote(dest, destall.at[me], d_send.at[o], d_recv.at[o], to)

    def cache_copy(o):
        to = lax.rem(me + o, peers)
        return remote(
            outgoing.at[pl.ds(to * per_peer, per_peer)],
            arrived.at[pl.ds(me * per_peer, per_peer)],
            c_send.at[o], c_recv.at[o], {"streams": to},
        )

    def frame_copy(o):
        to = {"mp": lax.rem(my + o, mps)}
        return remote(gathered.at[my], gathered.at[my], f_send.at[o], f_recv.at[o], to)

    def low_copy(o):
        to = {"mp": lax.rem(my + o, mps)}
        return remote(lows.at[my], lows.at[my], l_send.at[o], l_recv.at[o], to)

    def start_small(o, c):
        down_copy(o).start()
        return c

    def start_rest(o, c):
        up_copy(o).start()
        dest_copy(o).start()
        cache_copy(o).start()
        return c

    lax.fori_loop(1, peers, start_small, 0)
    for o in range(1, mps):
        frame_copy(o).start()
    lax.fori_loop(1, peers, start_rest, 0)

    downg[me] = down[...]
    upg[me] = up[...]
    destall[me] = dest[...]
    arrived[pl.ds(me * per_peer, per_peer)] = outgoing[pl.ds(me * per_peer, per_peer)]

    w_copy.wait()
    acc[...] = jnp.dot(
        mine, weight[pl.ds(pl.multiple_of(my * width, width), width), :],
        preferred_element_type=F32,
    )

    lane = iota((1, rows), 1) % count
    slot = jnp.zeros((1, rows), jnp.int32)
    for s in range(count):
        slot = jnp.where(lane == s, panel_s[tenant_s[s]], slot)

    def wait_down(o, c):
        down_copy(o).wait()
        return c

    lax.fori_loop(1, peers, wait_down, 0)
    panels = downg[...].reshape(peers * rank_dim, width)
    projected = lax.dot_general(
        panels, mine, (((1,), (1,)), ((), ())), preferred_element_type=F32
    )
    hit = iota((peers * rank_dim, rows), 0) // rank_dim == slot
    part = jnp.where(hit, projected, 0.0).reshape(peers, rank_dim, rows).sum(axis=0)
    lows[my] = part
    for o in range(1, mps):
        low_copy(o).start()

    def wait_small(o, c):
        dest_copy(o).wait()
        up_copy(o).wait()
        return c

    lax.fori_loop(1, peers, wait_small, 0)
    to_me = destall[:, 0, :] == me
    hits = jnp.where(to_me, 1.0, 0.0)
    tri = jnp.where(iota((128, 128), 0) < iota((128, 128), 1), 1.0, 0.0)
    earlier = jnp.dot(hits.astype(BF16), tri.astype(BF16), preferred_element_type=F32)
    owner = iota((peers, 128), 0).astype(F32)
    bucket = jnp.sum(hits * (owner * per_peer + earlier), axis=0, keepdims=True)
    eye = jnp.where(iota((128, 128), 0) == iota((128, 128), 1), 1.0, 0.0)
    column = lax.dot_general(
        eye.astype(BF16), jnp.broadcast_to(bucket, (128, 128)).astype(BF16),
        (((1,), (1,)), ((), ())), preferred_element_type=F32,
    )
    length = outgoing.shape[1]
    source = column[:count, :].astype(jnp.int32) * length

    for o in range(1, mps):
        low_copy(o).wait()
    low = lows[0]
    for j in range(1, mps):
        low = low + lows[j]
    low = low.astype(BF16).astype(F32)
    spread = jnp.where(
        hit, jnp.broadcast_to(low[None], (peers, rank_dim, rows)).reshape(peers * rank_dim, rows), 0.0
    )
    acc[...] += jnp.dot(
        spread.T.astype(BF16), upg[...].reshape(peers * rank_dim, 2 * width),
        preferred_element_type=F32,
    )

    for o in range(1, mps):
        frame_copy(o).wait()
        j = lax.rem(my + mps - o, mps)
        acc[...] += jnp.dot(
            gathered[j], weight[pl.ds(pl.multiple_of(j * width, width), width), :],
            preferred_element_type=F32,
        )
    pre = acc[...]
    gated = (pre[:, :width] * jax.nn.sigmoid(pre[:, width:])).astype(BF16)
    seq[pl.ds(hist, fr)] = gated.astype(F32).reshape(fr, count, width)

    def wait_cache(o, c):
        cache_copy(o).wait()
        return c

    lax.fori_loop(1, peers, wait_cache, 0)
    blocks = peers * per_peer * length
    flat = arrived[...].reshape(blocks, width)
    wanted = jnp.concatenate([source] * (blocks // 128), axis=1)
    wanted = wanted - iota((count, blocks), 1)
    select = jnp.concatenate(
        [jnp.where(wanted == -t, 1.0, 0.0).astype(BF16) for t in range(hist)], axis=0
    )
    moved = jnp.dot(select, flat, preferred_element_type=F32)
    seq[pl.ds(0, hist)] = moved.reshape(hist, count, width)

    limit = jnp.zeros((count, 128), jnp.int32)
    sub = iota((count, 128), 0)
    for s in range(count):
        limit = jnp.where(sub == s, valid_s[s] * CH, limit)
    seg = 8
    for sb in range(count // seg):
        keep = limit[sb * seg:(sb + 1) * seg][None] > iota((fr, seg, 128), 0)

        def column_block(cb, c, sb=sb, keep=keep):
            lanes = pl.ds(pl.multiple_of(cb * 128, 128), 128)
            total = jnp.zeros((fr, seg, 128), F32)
            for k in range(hist + 1):
                window = seq[pl.ds(k, fr), pl.ds(sb * seg, seg), lanes]
                total = total + window * taps[pl.ds(k, 1), lanes][None]
            normed = total * scale[:, lanes][None] + offset[:, lanes][None]
            active = normed * jax.nn.sigmoid(normed)
            enc[:, pl.ds(sb * seg, seg), lanes] = jnp.where(keep, active, 0.0)
            return c

        lax.fori_loop(0, width // 128, column_block, 0)
    back = jnp.where(r_i == (c_i % count) * fr + c_i // count, 1.0, 0.0).astype(BF16)
    out[...] = jnp.dot(
        back, enc[...].reshape(rows, width).astype(BF16), preferred_element_type=F32
    ).astype(BF16)


def local(
    frames, convolution_cache, destination, tenant, valid, tenant_panel_slot, input_weight,
    tenant_down_weight, tenant_up_weight, depthwise_taps, batchnorm_scale, batchnorm_offset,
):
    peers = lax.axis_size("streams")
    mps = lax.axis_size("mp")
    count = destination.shape[0]
    rows, width = frames.shape
    fr = rows // count
    hist = convolution_cache.shape[1]
    length = -(-hist // 16) * 16
    per_peer = max(1, count // peers)
    rank_dim = tenant_down_weight.shape[2]
    order = jnp.arange(count, dtype=jnp.int32)
    earlier = (destination[:, None] == destination[None, :]) & (order[None, :] < order[:, None])
    bucket = destination * per_peer + jnp.sum(earlier.astype(jnp.int32), axis=1)
    target = jnp.arange(peers * per_peer, dtype=jnp.int32)
    pick = jnp.sum(jnp.where(bucket[None, :] == target[:, None], order[None, :], 0), axis=1)
    dest = jnp.broadcast_to(
        jnp.pad(destination, (0, 128 - count), constant_values=-1)[None, :], (8, 128)
    )
    smem = pl.BlockSpec(memory_space=pltpu.SMEM)
    vmem = pl.BlockSpec(memory_space=pltpu.VMEM)
    dims = (peers, mps, count, fr, hist, width, per_peer, rank_dim)
    dma = pltpu.SemaphoreType.DMA
    return pl.pallas_call(
        functools.partial(kernel, dims),
        out_shape=jax.ShapeDtypeStruct((rows, width), BF16),
        in_specs=[smem] * 4 + [vmem] * 3 + [pl.BlockSpec(memory_space=pl.ANY)] + [vmem] * 5,
        out_specs=vmem,
        scratch_shapes=[
            pltpu.VMEM((mps, rows, width), BF16),
            pltpu.VMEM((peers * per_peer, length, width), BF16),
            pltpu.VMEM((peers * per_peer, length, width), BF16),
            pltpu.VMEM((peers, 8, 128), jnp.int32),
            pltpu.VMEM((peers, rank_dim, width), BF16),
            pltpu.VMEM((peers, rank_dim, 2 * width), BF16),
            pltpu.VMEM((mps, rank_dim, rows), F32),
            pltpu.VMEM((mps * width, 2 * width), BF16),
            pltpu.VMEM((rows, 2 * width), F32),
            pltpu.VMEM((hist + fr, count, width), F32),
            pltpu.VMEM((fr, count, width), F32),
            dma,
            dma((mps,)), dma((mps,)),
            dma((peers,)), dma((peers,)),
            dma((peers,)), dma((peers,)),
            dma((peers,)), dma((peers,)),
            dma((peers,)), dma((peers,)),
            dma((mps,)), dma((mps,)),
        ],
        compiler_params=pltpu.CompilerParams(
            collective_id=0, has_side_effects=True, vmem_limit_bytes=56 * 1024 * 1024
        ),
    )(
        pick, tenant, valid, tenant_panel_slot,
        frames, convolution_cache, dest,
        input_weight.reshape(mps * width, 2 * width),
        tenant_down_weight[0].T, tenant_up_weight.reshape(rank_dim, 2 * width),
        depthwise_taps, batchnorm_scale.reshape(1, width), batchnorm_offset.reshape(1, width),
    )


def solution(mesh):
    in_specs = (
        P("streams", "mp"),
        P("streams", None, "mp"),
        P("streams"),
        P("streams"),
        P("streams"),
        P(),
        P(None, None, "mp"),
        P("streams", "mp", None),
        P("streams", None, None, "mp"),
        P(None, "mp"),
        P("mp"),
        P("mp"),
    )
    return jax.shard_map(
        local, mesh=mesh, in_specs=in_specs, out_specs=P("streams", "mp"), check_vma=False
    )
```

```python
import functools

import jax
import jax.numpy as jnp
from jax import lax
from jax.experimental import pallas as pl
from jax.experimental.pallas import tpu as pltpu
from jax.sharding import PartitionSpec as P

CH = 3
MESH = pl.DeviceIdType.MESH
F32 = jnp.float32
BF16 = jnp.bfloat16


def iota(shape, dim):
    return lax.broadcasted_iota(jnp.int32, shape, dim)


def kernel(
    dims,
    dest_s, tenant_s, valid_s, panel_s,
    frames, cache, weight_hbm, down, up, taps, scale, offset,
    out,
    gathered, outgoing, arrived, dest, destall, select, downg, upg, lows, weight, acc, seq, enc,
    w_sem, f_send, f_recv, c_send, c_recv, d_send, d_recv, a_send, a_recv, u_send, u_recv,
    l_send, l_recv,
):
    peers, mps, count, fr, hist, length, width, per_peer, rank_dim = dims
    rows = count * fr
    me = lax.axis_index("streams")
    my = lax.axis_index("mp")

    w_copy = pltpu.make_async_copy(weight_hbm, weight, w_sem)
    w_copy.start()

    barrier = pltpu.get_barrier_semaphore()
    for o in range(1, mps):
        pl.semaphore_signal(
            barrier, inc=1, device_id={"mp": lax.rem(my + o, mps)}, device_id_type=MESH
        )

    def greet(o, c):
        pl.semaphore_signal(
            barrier, inc=1, device_id={"streams": lax.rem(me + o, peers)}, device_id_type=MESH
        )
        return c

    lax.fori_loop(1, peers, greet, 0)

    r_i, c_i = iota((rows, rows), 0), iota((rows, rows), 1)
    perm = jnp.where(c_i == (r_i % count) * fr + r_i // count, 1.0, 0.0).astype(BF16)
    mine = jnp.dot(perm, frames[...], preferred_element_type=F32).astype(BF16)
    gathered[my] = mine

    stream = iota((8, 128), 1) % count
    goes = jnp.zeros((8, 128), jnp.int32)
    for s in range(count):
        goes = jnp.where(stream == s, dest_s[s], goes)
    dest[...] = goes
    place = jnp.zeros((8, 128), jnp.int32)
    for s in range(count):
        place = place + jnp.where((goes == dest_s[s]) & (stream > s), 1, 0)
    chunk = length * per_peer
    key = (goes * chunk + place)[:1]
    lanes_all = hist * count
    wide = -(-lanes_all // 128)
    key = jnp.concatenate([key] * wide, axis=1)[:, :lanes_all]
    key = key + (iota((1, lanes_all), 1) // count) * per_peer

    pl.semaphore_wait(barrier, peers - 1 + mps - 1)

    def remote(src, dst, send, recv, where):
        return pltpu.make_async_remote_copy(
            src_ref=src, dst_ref=dst, send_sem=send, recv_sem=recv,
            device_id=where, device_id_type=MESH,
        )

    def down_copy(o):
        to = {"streams": lax.rem(me + o, peers)}
        return remote(down, downg.at[me], a_send.at[o], a_recv.at[o], to)

    def up_copy(o):
        to = {"streams": lax.rem(me + o, peers)}
        return remote(up, upg.at[me], u_send.at[o], u_recv.at[o], to)

    def dest_copy(o):
        to = {"streams": lax.rem(me + o, peers)}
        return remote(dest, destall.at[me], d_send.at[o], d_recv.at[o], to)

    def cache_copy(o):
        to = lax.rem(me + o, peers)
        return remote(
            outgoing.at[to], arrived.at[me],
            c_send.at[o], c_recv.at[o], {"streams": to},
        )

    def frame_copy(o):
        to = {"mp": lax.rem(my + o, mps)}
        return remote(gathered.at[my], gathered.at[my], f_send.at[o], f_recv.at[o], to)

    def low_copy(o):
        to = {"mp": lax.rem(my + o, mps)}
        return remote(lows.at[my], lows.at[my], l_send.at[o], l_recv.at[o], to)

    def start_small(o, c):
        down_copy(o).start()
        dest_copy(o).start()
        return c

    def start_rest(o, c):
        q = lax.rem(me + o, peers)
        rows_q = iota((chunk, lanes_all), 0) + q * chunk
        sel = jnp.where(rows_q == key, 1.0, 0.0).astype(BF16)
        outgoing[q] = jnp.dot(
            sel, cache[...].reshape(lanes_all, width), preferred_element_type=F32
        ).astype(BF16)

        @pl.when(o < peers)
        def _():
            cache_copy(o).start()

        return c

    lax.fori_loop(1, peers, start_small, 0)
    for o in range(1, mps):
        frame_copy(o).start()
    lax.fori_loop(1, peers + 1, start_rest, 0)

    def start_up(o, c):
        up_copy(o).start()
        return c

    lax.fori_loop(1, peers, start_up, 0)

    downg[me] = down[...]
    upg[me] = up[...]
    destall[me] = dest[...]
    arrived[me] = outgoing[me]

    w_copy.wait()
    acc[...] = jnp.dot(
        mine, weight[pl.ds(pl.multiple_of(my * width, width), width), :],
        preferred_element_type=F32,
    )

    lane = iota((1, rows), 1) % count
    slot = jnp.zeros((1, rows), jnp.int32)
    for s in range(count):
        slot = jnp.where(lane == s, panel_s[tenant_s[s]], slot)

    def wait_down(o, c):
        down_copy(o).wait()
        return c

    lax.fori_loop(1, peers, wait_down, 0)
    panels = downg[...].reshape(peers * rank_dim, width)
    projected = lax.dot_general(
        panels, mine, (((1,), (1,)), ((), ())), preferred_element_type=F32
    )
    hit = iota((peers * rank_dim, rows), 0) // rank_dim == slot
    part = jnp.where(hit, projected, 0.0).reshape(peers, rank_dim, rows).sum(axis=0)
    lows[my] = part
    for o in range(1, mps):
        low_copy(o).start()

    def wait_small(o, c):
        dest_copy(o).wait()
        up_copy(o).wait()
        return c

    lax.fori_loop(1, peers, wait_small, 0)
    to_me = (destall[:, 0, :] == me) & (iota((peers, 128), 1) < count)
    hits = jnp.where(to_me, 1.0, 0.0)
    tri = jnp.where(iota((128, 128), 0) < iota((128, 128), 1), 1.0, 0.0)
    earlier = jnp.dot(hits.astype(BF16), tri.astype(BF16), preferred_element_type=F32)
    owner = iota((peers, 128), 0).astype(F32)
    bucket = jnp.sum(hits * (owner * per_peer + earlier), axis=0, keepdims=True)
    eye = jnp.where(iota((128, 128), 0) == iota((128, 128), 1), 1.0, 0.0)
    column = lax.dot_general(
        eye.astype(BF16), jnp.broadcast_to(bucket, (128, 128)).astype(BF16),
        (((1,), (1,)), ((), ())), preferred_element_type=F32,
    )
    found = column[:count, :].astype(jnp.int32)
    source = (found // per_peer) * chunk + found % per_peer
    blocks = peers * chunk
    wanted = jnp.concatenate([source] * (blocks // 128), axis=1)
    wanted = iota((count, blocks), 1) - wanted
    for t in range(hist):
        select[t] = jnp.where(wanted == t * per_peer, 1.0, 0.0).astype(BF16)

    for o in range(1, mps):
        low_copy(o).wait()
    low = lows[0]
    for j in range(1, mps):
        low = low + lows[j]
    low = low.astype(BF16).astype(F32)
    spread = jnp.where(
        hit, jnp.broadcast_to(low[None], (peers, rank_dim, rows)).reshape(peers * rank_dim, rows), 0.0
    )
    acc[...] += jnp.dot(
        spread.T.astype(BF16), upg[...].reshape(peers * rank_dim, 2 * width),
        preferred_element_type=F32,
    )

    for o in range(1, mps):
        frame_copy(o).wait()
        j = lax.rem(my + mps - o, mps)
        acc[...] += jnp.dot(
            gathered[j], weight[pl.ds(pl.multiple_of(j * width, width), width), :],
            preferred_element_type=F32,
        )
    pre = acc[...]
    gated = (pre[:, :width] * jax.nn.sigmoid(pre[:, width:])).astype(BF16)
    seq[pl.ds(hist, fr)] = gated.astype(F32).reshape(fr, count, width)

    def wait_cache(o, c):
        cache_copy(o).wait()
        return c

    lax.fori_loop(1, peers, wait_cache, 0)
    moved = jnp.dot(
        select[...].reshape(lanes_all, blocks), arrived[...].reshape(blocks, width),
        preferred_element_type=F32,
    )
    seq[pl.ds(0, hist)] = moved.reshape(hist, count, width)

    limit = jnp.zeros((count, 128), jnp.int32)
    sub = iota((count, 128), 0)
    for s in range(count):
        limit = jnp.where(sub == s, valid_s[s] * CH, limit)
    seg = 8
    for sb in range(count // seg):
        keep = limit[sb * seg:(sb + 1) * seg][None] > iota((fr, seg, 128), 0)

        def column_block(cb, c, sb=sb, keep=keep):
            lanes = pl.ds(pl.multiple_of(cb * 128, 128), 128)
            total = jnp.zeros((fr, seg, 128), F32)
            for k in range(hist + 1):
                window = seq[pl.ds(k, fr), pl.ds(sb * seg, seg), lanes]
                total = total + window * taps[pl.ds(k, 1), lanes][None]
            normed = total * scale[lanes].reshape(1, 1, 128) + offset[lanes].reshape(1, 1, 128)
            active = normed * jax.nn.sigmoid(normed)
            enc[:, pl.ds(sb * seg, seg), lanes] = jnp.where(keep, active, 0.0)
            return c

        lax.fori_loop(0, width // 128, column_block, 0)
    back = jnp.where(r_i == (c_i % count) * fr + c_i // count, 1.0, 0.0).astype(BF16)
    out[...] = jnp.dot(
        back, enc[...].reshape(rows, width).astype(BF16), preferred_element_type=F32
    ).astype(BF16)


def local(
    frames, convolution_cache, destination, tenant, valid, tenant_panel_slot, input_weight,
    tenant_down_weight, tenant_up_weight, depthwise_taps, batchnorm_scale, batchnorm_offset,
):
    peers = lax.axis_size("streams")
    mps = lax.axis_size("mp")
    count = destination.shape[0]
    rows, width = frames.shape
    fr = rows // count
    hist = convolution_cache.shape[1]
    length = -(-hist // 16) * 16
    per_peer = max(1, count // peers)
    rank_dim = tenant_down_weight.shape[2]
    smem = pl.BlockSpec(memory_space=pltpu.SMEM)
    vmem = pl.BlockSpec(memory_space=pltpu.VMEM)
    dims = (peers, mps, count, fr, hist, length, width, per_peer, rank_dim)
    dma = pltpu.SemaphoreType.DMA
    return pl.pallas_call(
        functools.partial(kernel, dims),
        out_shape=jax.ShapeDtypeStruct((rows, width), BF16),
        in_specs=[smem] * 4 + [vmem] * 2 + [pl.BlockSpec(memory_space=pl.ANY)] + [vmem] * 5,
        out_specs=vmem,
        scratch_shapes=[
            pltpu.VMEM((mps, rows, width), BF16),
            pltpu.VMEM((peers, length * per_peer, width), BF16),
            pltpu.VMEM((peers, length * per_peer, width), BF16),
            pltpu.VMEM((8, 128), jnp.int32),
            pltpu.VMEM((peers, 8, 128), jnp.int32),
            pltpu.VMEM((hist, count, peers * length * per_peer), BF16),
            pltpu.VMEM((peers, rank_dim, width), BF16),
            pltpu.VMEM((peers, rank_dim, 2 * width), BF16),
            pltpu.VMEM((mps, rank_dim, rows), F32),
            pltpu.VMEM((mps * width, 2 * width), BF16),
            pltpu.VMEM((rows, 2 * width), F32),
            pltpu.VMEM((hist + fr, count, width), F32),
            pltpu.VMEM((fr, count, width), F32),
            dma,
            dma((mps,)), dma((mps,)),
            dma((peers,)), dma((peers,)),
            dma((peers,)), dma((peers,)),
            dma((peers,)), dma((peers,)),
            dma((peers,)), dma((peers,)),
            dma((mps,)), dma((mps,)),
        ],
        compiler_params=pltpu.CompilerParams(
            collective_id=0, has_side_effects=True, vmem_limit_bytes=56 * 1024 * 1024
        ),
    )(
        destination, tenant, valid, tenant_panel_slot,
        frames, convolution_cache.transpose(1, 0, 2),
        input_weight.reshape(mps * width, 2 * width),
        tenant_down_weight[0].T, tenant_up_weight.reshape(rank_dim, 2 * width),
        depthwise_taps, batchnorm_scale, batchnorm_offset,
    )


def solution(mesh):
    in_specs = (
        P("streams", "mp"),
        P("streams", None, "mp"),
        P("streams"),
        P("streams"),
        P("streams"),
        P(),
        P(None, None, "mp"),
        P("streams", "mp", None),
        P("streams", None, None, "mp"),
        P(None, "mp"),
        P("mp"),
        P("mp"),
    )
    return jax.shard_map(
        local, mesh=mesh, in_specs=in_specs, out_specs=P("streams", "mp"), check_vma=False
    )
```

```python
import functools

import jax
import jax.numpy as jnp
from jax import lax
from jax.experimental import pallas as pl
from jax.experimental.pallas import tpu as pltpu
from jax.sharding import PartitionSpec as P

CH = 3
MESH = pl.DeviceIdType.MESH
F32 = jnp.float32
BF16 = jnp.bfloat16


def iota(shape, dim):
    return lax.broadcasted_iota(jnp.int32, shape, dim)


def kernel(
    dims,
    dest_s, tenant_s, valid_s, panel_s,
    frames, cache, weight_hbm, down, up_raw, taps, scale, offset,
    out,
    gathered, outgoing, arrived, dest, destall, select, downg, upg, lows, up, cache32, raw, weight, acc, seq, enc,
    w_sem, f_send, f_recv, c_send, c_recv, d_send, d_recv, a_send, a_recv, u_send, u_recv,
    l_send, l_recv,
):
    peers, mps, count, fr, hist, length, width, per_peer, rank_dim = dims
    rows = count * fr
    me = lax.axis_index("streams")
    my = lax.axis_index("mp")

    w_copy = pltpu.make_async_copy(weight_hbm, raw, w_sem)
    w_copy.start()

    barrier = pltpu.get_barrier_semaphore()
    for o in range(1, mps):
        pl.semaphore_signal(
            barrier, inc=1, device_id={"mp": lax.rem(my + o, mps)}, device_id_type=MESH
        )

    def greet(o, c):
        pl.semaphore_signal(
            barrier, inc=1, device_id={"streams": lax.rem(me + o, peers)}, device_id_type=MESH
        )
        return c

    lax.fori_loop(1, peers, greet, 0)

    r_i, c_i = iota((rows, rows), 0), iota((rows, rows), 1)
    perm = jnp.where(c_i == (r_i % count) * fr + r_i // count, 1.0, 0.0).astype(BF16)
    mine = jnp.dot(perm, frames[...], preferred_element_type=F32).astype(BF16)
    gathered[my] = mine
    halves = up_raw[...].astype(F32)
    up[:, :width] = halves[:, 0, :].astype(BF16)
    up[:, width:] = halves[:, 1, :].astype(BF16)
    for j in range(width // 128):
        piece = cache[:, :, j * 128:(j + 1) * 128].reshape(hist * count, 128)
        cache32[j] = piece.astype(F32)
    blank = jnp.zeros((length - hist, width), F32)

    stream = iota((8, 128), 1) % count
    goes = jnp.zeros((8, 128), jnp.int32)
    for s in range(count):
        goes = jnp.where(stream == s, dest_s[s], goes)
    dest[...] = goes
    chunk = length * per_peer

    pl.semaphore_wait(barrier, peers - 1 + mps - 1)

    def remote(src, dst, send, recv, where):
        return pltpu.make_async_remote_copy(
            src_ref=src, dst_ref=dst, send_sem=send, recv_sem=recv,
            device_id=where, device_id_type=MESH,
        )

    def down_copy(o):
        to = {"streams": lax.rem(me + o, peers)}
        return remote(down, downg.at[me], a_send.at[o], a_recv.at[o], to)

    def up_copy(o):
        to = {"streams": lax.rem(me + o, peers)}
        return remote(up, upg.at[me], u_send.at[o], u_recv.at[o], to)

    def dest_copy(o):
        to = {"streams": lax.rem(me + o, peers)}
        return remote(dest, destall.at[me], d_send.at[o], d_recv.at[o], to)

    def cache_copy(o):
        to = lax.rem(me + o, peers)
        return remote(
            outgoing.at[to], arrived.at[me],
            c_send.at[o], c_recv.at[o], {"streams": to},
        )

    def frame_copy(o):
        to = {"mp": lax.rem(my + o, mps)}
        return remote(gathered.at[my], gathered.at[my], f_send.at[o], f_recv.at[o], to)

    def low_copy(o):
        to = {"mp": lax.rem(my + o, mps)}
        return remote(lows.at[my], lows.at[my], l_send.at[o], l_recv.at[o], to)

    def start_small(o, c):
        down_copy(o).start()
        dest_copy(o).start()
        return c

    def start_rest(o, c):
        q = lax.rem(me + o, peers)
        picks = [jnp.int32(0)] * per_peer
        for s in reversed(range(count)):
            fits = dest_s[s] == q
            picks = [
                jnp.where(fits, new, old) for new, old in zip([jnp.int32(s)] + picks[:-1], picks)
            ]
        for r, p in enumerate(picks):
            one = jnp.concatenate(
                [
                    cache32.at[j][pl.ds(p, hist, stride=count), :]
                    for j in range(width // 128)
                ],
                axis=1,
            )
            outgoing[q, r * length:(r + 1) * length, :] = jnp.concatenate(
                [one, blank], axis=0
            ).astype(BF16)

        @pl.when(o < peers)
        def _():
            cache_copy(o).start()

        return c

    lax.fori_loop(1, peers, start_small, 0)
    for o in range(1, mps):
        frame_copy(o).start()
    lax.fori_loop(1, peers + 1, start_rest, 0)

    def start_up(o, c):
        up_copy(o).start()
        return c

    lax.fori_loop(1, peers, start_up, 0)

    downg[me] = down[...]
    upg[me] = up[...]
    destall[me] = dest[...]
    arrived[me] = outgoing[me]

    w_copy.wait()

    def split(i, c):
        at = pl.ds(pl.multiple_of(i * 64, 64), 64)
        both = raw[at].astype(F32)
        weight[at, :width] = both[:, 0, :].astype(BF16)
        weight[at, width:] = both[:, 1, :].astype(BF16)
        return c

    lax.fori_loop(0, mps * width // 64, split, 0)
    acc[...] = jnp.dot(
        mine, weight[pl.ds(pl.multiple_of(my * width, width), width), :],
        preferred_element_type=F32,
    )

    lane = iota((1, rows), 1) % count
    slot = jnp.zeros((1, rows), jnp.int32)
    for s in range(count):
        slot = jnp.where(lane == s, panel_s[tenant_s[s]], slot)

    def wait_down(o, c):
        down_copy(o).wait()
        return c

    lax.fori_loop(1, peers, wait_down, 0)
    panels = downg[...].reshape(peers * rank_dim, width)
    projected = lax.dot_general(
        panels, mine, (((1,), (1,)), ((), ())), preferred_element_type=F32
    )
    hit = iota((peers * rank_dim, rows), 0) // rank_dim == slot
    part = jnp.where(hit, projected, 0.0).reshape(peers, rank_dim, rows).sum(axis=0)
    lows[my] = part
    for o in range(1, mps):
        low_copy(o).start()

    def wait_small(o, c):
        dest_copy(o).wait()
        up_copy(o).wait()
        return c

    lax.fori_loop(1, peers, wait_small, 0)
    to_me = (destall[:, 0, :] == me) & (iota((peers, 128), 1) < count)
    hits = jnp.where(to_me, 1.0, 0.0)
    tri = jnp.where(iota((128, 128), 0) < iota((128, 128), 1), 1.0, 0.0)
    earlier = jnp.dot(hits.astype(BF16), tri.astype(BF16), preferred_element_type=F32)
    owner = iota((peers, 128), 0).astype(F32)
    bucket = jnp.sum(hits * (owner * per_peer + earlier), axis=0, keepdims=True)
    eye = jnp.where(iota((128, 128), 0) == iota((128, 128), 1), 1.0, 0.0)
    column = lax.dot_general(
        eye.astype(BF16), jnp.broadcast_to(bucket, (128, 128)).astype(BF16),
        (((1,), (1,)), ((), ())), preferred_element_type=F32,
    )
    found = column[:count, :].astype(jnp.int32)
    source = found * length
    blocks = peers * chunk
    lanes_all = hist * count
    wanted = jnp.concatenate([source] * (blocks // 128), axis=1)
    wanted = iota((count, blocks), 1) - wanted
    for t in range(hist):
        select[t] = jnp.where(wanted == t, 1.0, 0.0).astype(BF16)

    for o in range(1, mps):
        low_copy(o).wait()
    low = lows[0]
    for j in range(1, mps):
        low = low + lows[j]
    low = low.astype(BF16).astype(F32)
    spread = jnp.where(
        hit, jnp.broadcast_to(low[None], (peers, rank_dim, rows)).reshape(peers * rank_dim, rows), 0.0
    )
    acc[...] += jnp.dot(
        spread.T.astype(BF16), upg[...].reshape(peers * rank_dim, 2 * width),
        preferred_element_type=F32,
    )

    for o in range(1, mps):
        frame_copy(o).wait()
        j = lax.rem(my + mps - o, mps)
        acc[...] += jnp.dot(
            gathered[j], weight[pl.ds(pl.multiple_of(j * width, width), width), :],
            preferred_element_type=F32,
        )
    pre = acc[...]
    gated = (pre[:, :width] * jax.nn.sigmoid(pre[:, width:])).astype(BF16)
    seq[pl.ds(hist, fr)] = gated.astype(F32).reshape(fr, count, width)

    def wait_cache(o, c):
        cache_copy(o).wait()
        return c

    lax.fori_loop(1, peers, wait_cache, 0)
    moved = jnp.dot(
        select[...].reshape(lanes_all, blocks), arrived[...].reshape(blocks, width),
        preferred_element_type=F32,
    )
    seq[pl.ds(0, hist)] = moved.reshape(hist, count, width)

    limit = jnp.zeros((count, 128), jnp.int32)
    sub = iota((count, 128), 0)
    for s in range(count):
        limit = jnp.where(sub == s, valid_s[s] * CH, limit)
    seg = 8
    for sb in range(count // seg):
        keep = limit[sb * seg:(sb + 1) * seg][None] > iota((fr, seg, 128), 0)

        def column_block(cb, c, sb=sb, keep=keep):
            lanes = pl.ds(pl.multiple_of(cb * 128, 128), 128)
            total = jnp.zeros((fr, seg, 128), F32)
            for k in range(hist + 1):
                window = seq[pl.ds(k, fr), pl.ds(sb * seg, seg), lanes]
                total = total + window * taps[pl.ds(k, 1), lanes][None]
            normed = total * scale[lanes].reshape(1, 1, 128) + offset[lanes].reshape(1, 1, 128)
            active = normed * jax.nn.sigmoid(normed)
            enc[:, pl.ds(sb * seg, seg), lanes] = jnp.where(keep, active, 0.0)
            return c

        lax.fori_loop(0, width // 128, column_block, 0)
    back = jnp.where(r_i == (c_i % count) * fr + c_i // count, 1.0, 0.0).astype(BF16)
    out[...] = jnp.dot(
        back, enc[...].reshape(rows, width).astype(BF16), preferred_element_type=F32
    ).astype(BF16)


def local(
    frames, convolution_cache, destination, tenant, valid, tenant_panel_slot, input_weight,
    tenant_down_weight, tenant_up_weight, depthwise_taps, batchnorm_scale, batchnorm_offset,
):
    peers = lax.axis_size("streams")
    mps = lax.axis_size("mp")
    count = destination.shape[0]
    rows, width = frames.shape
    fr = rows // count
    hist = convolution_cache.shape[1]
    length = -(-hist // 16) * 16
    per_peer = max(1, count // peers)
    rank_dim = tenant_down_weight.shape[2]
    smem = pl.BlockSpec(memory_space=pltpu.SMEM)
    vmem = pl.BlockSpec(memory_space=pltpu.VMEM)
    dims = (peers, mps, count, fr, hist, length, width, per_peer, rank_dim)
    dma = pltpu.SemaphoreType.DMA
    return pl.pallas_call(
        functools.partial(kernel, dims),
        out_shape=jax.ShapeDtypeStruct((rows, width), BF16),
        in_specs=[smem] * 4 + [vmem] * 2 + [pl.BlockSpec(memory_space=pl.ANY)] + [vmem] * 5,
        out_specs=vmem,
        scratch_shapes=[
            pltpu.VMEM((mps, rows, width), BF16),
            pltpu.VMEM((peers, length * per_peer, width), BF16),
            pltpu.VMEM((peers, length * per_peer, width), BF16),
            pltpu.VMEM((8, 128), jnp.int32),
            pltpu.VMEM((peers, 8, 128), jnp.int32),
            pltpu.VMEM((hist, count, peers * length * per_peer), BF16),
            pltpu.VMEM((peers, rank_dim, width), BF16),
            pltpu.VMEM((peers, rank_dim, 2 * width), BF16),
            pltpu.VMEM((mps, rank_dim, rows), F32),
            pltpu.VMEM((rank_dim, 2 * width), BF16),
            pltpu.VMEM((width // 128, hist * count, 128), F32),
            pltpu.VMEM((mps * width, 2, width), BF16),
            pltpu.VMEM((mps * width, 2 * width), BF16),
            pltpu.VMEM((rows, 2 * width), F32),
            pltpu.VMEM((hist + fr, count, width), F32),
            pltpu.VMEM((fr, count, width), F32),
            dma,
            dma((mps,)), dma((mps,)),
            dma((peers,)), dma((peers,)),
            dma((peers,)), dma((peers,)),
            dma((peers,)), dma((peers,)),
            dma((peers,)), dma((peers,)),
            dma((mps,)), dma((mps,)),
        ],
        compiler_params=pltpu.CompilerParams(
            collective_id=0, has_side_effects=True, vmem_limit_bytes=56 * 1024 * 1024
        ),
    )(
        destination, tenant, valid, tenant_panel_slot,
        frames, convolution_cache.transpose(1, 0, 2),
        input_weight,
        tenant_down_weight[0].T, tenant_up_weight[0],
        depthwise_taps, batchnorm_scale, batchnorm_offset,
    )


def solution(mesh):
    in_specs = (
        P("streams", "mp"),
        P("streams", None, "mp"),
        P("streams"),
        P("streams"),
        P("streams"),
        P(),
        P(None, None, "mp"),
        P("streams", "mp", None),
        P("streams", None, None, "mp"),
        P(None, "mp"),
        P("mp"),
        P("mp"),
    )
    return jax.shard_map(
        local, mesh=mesh, in_specs=in_specs, out_specs=P("streams", "mp"), check_vma=False
    )
```

```python
import functools

import jax
import jax.numpy as jnp
from jax import lax
from jax.experimental import pallas as pl
from jax.experimental.pallas import tpu as pltpu
from jax.sharding import PartitionSpec as P

CH = 3
MESH = pl.DeviceIdType.MESH
F32 = jnp.float32
BF16 = jnp.bfloat16


def iota(shape, dim):
    return lax.broadcasted_iota(jnp.int32, shape, dim)


def kernel(
    dims,
    dest_s, tenant_s, valid_s, panel_s,
    frames, cache, weight_hbm, down, up_raw, taps, scale, offset,
    out,
    gathered, outgoing, arrived, dest, destall, select, downg, upg, lows, up, cache32, raw, weight, acc, seq, enc,
    w_sem, f_send, f_recv, c_send, c_recv, g_send, g_recv,
    l_send, l_recv,
):
    peers, mps, count, fr, hist, length, width, per_peer, rank_dim = dims
    rows = count * fr
    me = lax.axis_index("streams")
    my = lax.axis_index("mp")

    w_copy = pltpu.make_async_copy(weight_hbm, raw, w_sem)
    w_copy.start()

    barrier = pltpu.get_barrier_semaphore()
    for o in range(1, mps):
        pl.semaphore_signal(
            barrier, inc=1, device_id={"mp": lax.rem(my + o, mps)}, device_id_type=MESH
        )

    def greet(o, c):
        pl.semaphore_signal(
            barrier, inc=1, device_id={"streams": lax.rem(me + o, peers)}, device_id_type=MESH
        )
        return c

    lax.fori_loop(1, peers, greet, 0)

    r_i, c_i = iota((rows, rows), 0), iota((rows, rows), 1)
    perm = jnp.where(c_i == (r_i % count) * fr + r_i // count, 1.0, 0.0).astype(BF16)
    mine = jnp.dot(perm, frames[...], preferred_element_type=F32).astype(BF16)
    gathered[my] = mine
    halves = up_raw[...].astype(F32)
    up[:, :width] = halves[:, 0, :].astype(BF16)
    up[:, width:] = halves[:, 1, :].astype(BF16)
    for j in range(width // 128):
        piece = cache[:, :, j * 128:(j + 1) * 128].reshape(hist * count, 128)
        cache32[j] = piece.astype(F32)
    blank = jnp.zeros((length - hist, width), F32)

    stream = iota((8, 128), 1) % count
    goes = jnp.zeros((8, 128), jnp.int32)
    for s in range(count):
        goes = jnp.where(stream == s, dest_s[s], goes)
    dest[...] = goes
    chunk = length * per_peer

    pl.semaphore_wait(barrier, peers - 1 + mps - 1)

    def remote(src, dst, send, recv, where):
        return pltpu.make_async_remote_copy(
            src_ref=src, dst_ref=dst, send_sem=send, recv_sem=recv,
            device_id=where, device_id_type=MESH,
        )

    half = peers // 2
    side, place = lax.rem(me, 2), me // 2
    pair = {"streams": me + 1 - 2 * side}
    small = ((down, downg), (dest, destall), (up, upg))

    def small_copy(i, o):
        src, dst = small[i]
        to = {"streams": 2 * lax.rem(place + o, half) + side}
        return remote(src, dst.at[side, place], g_send.at[i, o], g_recv.at[i, o], to)

    def pair_copy(i):
        dst = small[i][1]
        return remote(dst.at[side], dst.at[side], g_send.at[i, 0], g_recv.at[i, 0], pair)

    def relay(i):
        def arrive(o, c):
            small_copy(i, o).wait()
            return c

        lax.fori_loop(1, half, arrive, 0)
        pair_copy(i).start()

    def cache_copy(o):
        to = lax.rem(me + o, peers)
        return remote(
            outgoing.at[to], arrived.at[me],
            c_send.at[o], c_recv.at[o], {"streams": to},
        )

    def frame_copy(o):
        to = {"mp": lax.rem(my + o, mps)}
        return remote(gathered.at[my], gathered.at[my], f_send.at[o], f_recv.at[o], to)

    def low_copy(o):
        to = {"mp": lax.rem(my + o, mps)}
        return remote(lows.at[my], lows.at[my], l_send.at[o], l_recv.at[o], to)

    downg[side, place] = down[...]
    destall[side, place] = dest[...]
    upg[side, place] = up[...]

    def start_small(o, c):
        for i in range(3):
            small_copy(i, o).start()
        return c

    lax.fori_loop(1, half, start_small, 0)

    def start_rest(o, c):
        q = lax.rem(me + o, peers)
        picks = [jnp.int32(0)] * per_peer
        for s in reversed(range(count)):
            fits = dest_s[s] == q
            picks = [
                jnp.where(fits, new, old) for new, old in zip([jnp.int32(s)] + picks[:-1], picks)
            ]
        for r, p in enumerate(picks):
            one = jnp.concatenate(
                [
                    cache32.at[j][pl.ds(p, hist, stride=count), :]
                    for j in range(width // 128)
                ],
                axis=1,
            )
            outgoing[q, r * length:(r + 1) * length, :] = jnp.concatenate(
                [one, blank], axis=0
            ).astype(BF16)

        @pl.when(o < peers)
        def _():
            cache_copy(o).start()

        return c

    for o in range(1, mps):
        frame_copy(o).start()
    lax.fori_loop(1, peers + 1, start_rest, 0)

    arrived[me] = outgoing[me]
    for i in range(3):
        relay(i)

    w_copy.wait()

    def split(i, c):
        at = pl.ds(pl.multiple_of(i * 64, 64), 64)
        both = raw[at].astype(F32)
        weight[at, :width] = both[:, 0, :].astype(BF16)
        weight[at, width:] = both[:, 1, :].astype(BF16)
        return c

    lax.fori_loop(0, mps * width // 64, split, 0)
    acc[...] = jnp.dot(
        mine, weight[pl.ds(pl.multiple_of(my * width, width), width), :],
        preferred_element_type=F32,
    )

    lane = iota((1, rows), 1) % count
    slot = jnp.zeros((1, rows), jnp.int32)
    for s in range(count):
        slot = jnp.where(lane == s, panel_s[tenant_s[s]], slot)

    for i in range(3):
        pair_copy(i).wait()
    panels = downg[...].reshape(peers * rank_dim, width)
    projected = lax.dot_general(
        panels, mine, (((1,), (1,)), ((), ())), preferred_element_type=F32
    )
    at = iota((peers * rank_dim, rows), 0) // rank_dim
    hit = at == (slot % 2) * half + slot // 2
    part = jnp.where(hit, projected, 0.0).reshape(peers, rank_dim, rows).sum(axis=0)
    lows[my] = part
    for o in range(1, mps):
        low_copy(o).start()

    to_me = (destall[...].reshape(peers, 8, 128)[:, 0, :] == me) & (iota((peers, 128), 1) < count)
    hits = jnp.where(to_me, 1.0, 0.0)
    tri = jnp.where(iota((128, 128), 0) < iota((128, 128), 1), 1.0, 0.0)
    earlier = jnp.dot(hits.astype(BF16), tri.astype(BF16), preferred_element_type=F32)
    at = iota((peers, 128), 0)
    owner = (2 * (at % half) + at // half).astype(F32)
    bucket = jnp.sum(hits * (owner * per_peer + earlier), axis=0, keepdims=True)
    eye = jnp.where(iota((128, 128), 0) == iota((128, 128), 1), 1.0, 0.0)
    column = lax.dot_general(
        eye.astype(BF16), jnp.broadcast_to(bucket, (128, 128)).astype(BF16),
        (((1,), (1,)), ((), ())), preferred_element_type=F32,
    )
    found = column[:count, :].astype(jnp.int32)
    source = found * length
    blocks = peers * chunk
    lanes_all = hist * count
    wanted = jnp.concatenate([source] * (blocks // 128), axis=1)
    wanted = iota((count, blocks), 1) - wanted
    for t in range(hist):
        select[t] = jnp.where(wanted == t, 1.0, 0.0).astype(BF16)

    for o in range(1, mps):
        low_copy(o).wait()
    low = lows[0]
    for j in range(1, mps):
        low = low + lows[j]
    low = low.astype(BF16).astype(F32)
    spread = jnp.where(
        hit, jnp.broadcast_to(low[None], (peers, rank_dim, rows)).reshape(peers * rank_dim, rows), 0.0
    )
    acc[...] += jnp.dot(
        spread.T.astype(BF16), upg[...].reshape(peers * rank_dim, 2 * width),
        preferred_element_type=F32,
    )

    for o in range(1, mps):
        frame_copy(o).wait()
        j = lax.rem(my + mps - o, mps)
        acc[...] += jnp.dot(
            gathered[j], weight[pl.ds(pl.multiple_of(j * width, width), width), :],
            preferred_element_type=F32,
        )
    pre = acc[...]
    gated = (pre[:, :width] * jax.nn.sigmoid(pre[:, width:])).astype(BF16)
    seq[pl.ds(hist, fr)] = gated.astype(F32).reshape(fr, count, width)

    def wait_cache(o, c):
        cache_copy(o).wait()
        return c

    lax.fori_loop(1, peers, wait_cache, 0)
    moved = jnp.dot(
        select[...].reshape(lanes_all, blocks), arrived[...].reshape(blocks, width),
        preferred_element_type=F32,
    )
    seq[pl.ds(0, hist)] = moved.reshape(hist, count, width)

    limit = jnp.zeros((count, 128), jnp.int32)
    sub = iota((count, 128), 0)
    for s in range(count):
        limit = jnp.where(sub == s, valid_s[s] * CH, limit)
    seg = 8
    for sb in range(count // seg):
        keep = limit[sb * seg:(sb + 1) * seg][None] > iota((fr, seg, 128), 0)

        def column_block(cb, c, sb=sb, keep=keep):
            lanes = pl.ds(pl.multiple_of(cb * 128, 128), 128)
            total = jnp.zeros((fr, seg, 128), F32)
            for k in range(hist + 1):
                window = seq[pl.ds(k, fr), pl.ds(sb * seg, seg), lanes]
                total = total + window * taps[pl.ds(k, 1), lanes][None]
            normed = total * scale[lanes].reshape(1, 1, 128) + offset[lanes].reshape(1, 1, 128)
            active = normed * jax.nn.sigmoid(normed)
            enc[:, pl.ds(sb * seg, seg), lanes] = jnp.where(keep, active, 0.0)
            return c

        lax.fori_loop(0, width // 128, column_block, 0)
    back = jnp.where(r_i == (c_i % count) * fr + c_i // count, 1.0, 0.0).astype(BF16)
    out[...] = jnp.dot(
        back, enc[...].reshape(rows, width).astype(BF16), preferred_element_type=F32
    ).astype(BF16)


def local(
    frames, convolution_cache, destination, tenant, valid, tenant_panel_slot, input_weight,
    tenant_down_weight, tenant_up_weight, depthwise_taps, batchnorm_scale, batchnorm_offset,
):
    peers = lax.axis_size("streams")
    mps = lax.axis_size("mp")
    count = destination.shape[0]
    rows, width = frames.shape
    fr = rows // count
    hist = convolution_cache.shape[1]
    length = -(-hist // 16) * 16
    per_peer = max(1, count // peers)
    rank_dim = tenant_down_weight.shape[2]
    smem = pl.BlockSpec(memory_space=pltpu.SMEM)
    vmem = pl.BlockSpec(memory_space=pltpu.VMEM)
    dims = (peers, mps, count, fr, hist, length, width, per_peer, rank_dim)
    dma = pltpu.SemaphoreType.DMA
    return pl.pallas_call(
        functools.partial(kernel, dims),
        out_shape=jax.ShapeDtypeStruct((rows, width), BF16),
        in_specs=[smem] * 4 + [vmem] * 2 + [pl.BlockSpec(memory_space=pl.ANY)] + [vmem] * 5,
        out_specs=vmem,
        scratch_shapes=[
            pltpu.VMEM((mps, rows, width), BF16),
            pltpu.VMEM((peers, length * per_peer, width), BF16),
            pltpu.VMEM((peers, length * per_peer, width), BF16),
            pltpu.VMEM((8, 128), jnp.int32),
            pltpu.VMEM((2, peers // 2, 8, 128), jnp.int32),
            pltpu.VMEM((hist, count, peers * length * per_peer), BF16),
            pltpu.VMEM((2, peers // 2, rank_dim, width), BF16),
            pltpu.VMEM((2, peers // 2, rank_dim, 2 * width), BF16),
            pltpu.VMEM((mps, rank_dim, rows), F32),
            pltpu.VMEM((rank_dim, 2 * width), BF16),
            pltpu.VMEM((width // 128, hist * count, 128), F32),
            pltpu.VMEM((mps * width, 2, width), BF16),
            pltpu.VMEM((mps * width, 2 * width), BF16),
            pltpu.VMEM((rows, 2 * width), F32),
            pltpu.VMEM((hist + fr, count, width), F32),
            pltpu.VMEM((fr, count, width), F32),
            dma,
            dma((mps,)), dma((mps,)),
            dma((peers,)), dma((peers,)),
            dma((3, peers // 2)), dma((3, peers // 2)),
            dma((mps,)), dma((mps,)),
        ],
        compiler_params=pltpu.CompilerParams(
            collective_id=0, has_side_effects=True, vmem_limit_bytes=56 * 1024 * 1024
        ),
    )(
        destination, tenant, valid, tenant_panel_slot,
        frames, convolution_cache.transpose(1, 0, 2),
        input_weight,
        tenant_down_weight[0].T, tenant_up_weight[0],
        depthwise_taps, batchnorm_scale, batchnorm_offset,
    )


def solution(mesh):
    in_specs = (
        P("streams", "mp"),
        P("streams", None, "mp"),
        P("streams"),
        P("streams"),
        P("streams"),
        P(),
        P(None, None, "mp"),
        P("streams", "mp", None),
        P("streams", None, None, "mp"),
        P(None, "mp"),
        P("mp"),
        P("mp"),
    )
    return jax.shard_map(
        local, mesh=mesh, in_specs=in_specs, out_specs=P("streams", "mp"), check_vma=False
    )
```

```python
import functools

import jax
import jax.numpy as jnp
from jax import lax
from jax.experimental import pallas as pl
from jax.experimental.pallas import tpu as pltpu
from jax.sharding import PartitionSpec as P

CH = 3
MESH = pl.DeviceIdType.MESH
F32 = jnp.float32
BF16 = jnp.bfloat16


def iota(shape, dim):
    return lax.broadcasted_iota(jnp.int32, shape, dim)


def kernel(
    dims,
    dest_s, tenant_s, valid_s, panel_s,
    frames, cache, weight_hbm, down, up_raw, taps, scale, offset,
    out,
    gathered, outgoing, arrived, dest, destall, select, downg, upg, lows, up, cache32, raw, weight, acc, seq, enc,
    w_sem, f_send, f_recv, c_send, c_recv, g_send, g_recv,
    l_send, l_recv,
):
    peers, mps, count, fr, hist, length, width, per_peer, rank_dim = dims
    rows = count * fr
    me = lax.axis_index("streams")
    my = lax.axis_index("mp")

    w_copy = pltpu.make_async_copy(weight_hbm, raw, w_sem)
    w_copy.start()

    barrier = pltpu.get_barrier_semaphore()
    for o in range(1, mps):
        pl.semaphore_signal(
            barrier, inc=1, device_id={"mp": lax.rem(my + o, mps)}, device_id_type=MESH
        )

    def greet(o, c):
        pl.semaphore_signal(
            barrier, inc=1, device_id={"streams": lax.rem(me + o, peers)}, device_id_type=MESH
        )
        return c

    lax.fori_loop(1, peers, greet, 0)

    r_i, c_i = iota((rows, rows), 0), iota((rows, rows), 1)
    perm = jnp.where(c_i == (r_i % count) * fr + r_i // count, 1.0, 0.0).astype(BF16)
    mine = jnp.dot(perm, frames[...], preferred_element_type=F32).astype(BF16)
    gathered[my] = mine
    halves = up_raw[...].astype(F32)
    up[:, :width] = halves[:, 0, :].astype(BF16)
    up[:, width:] = halves[:, 1, :].astype(BF16)
    for j in range(width // 128):
        piece = cache[:, :, j * 128:(j + 1) * 128].reshape(hist * count, 128)
        cache32[j] = piece.astype(F32)
    blank = jnp.zeros((length - hist, width), F32)

    stream = iota((8, 128), 1) % count
    goes = jnp.zeros((8, 128), jnp.int32)
    for s in range(count):
        goes = jnp.where(stream == s, dest_s[s], goes)
    dest[...] = goes
    chunk = length * per_peer

    pl.semaphore_wait(barrier, peers - 1 + mps - 1)

    def remote(src, dst, send, recv, where):
        return pltpu.make_async_remote_copy(
            src_ref=src, dst_ref=dst, send_sem=send, recv_sem=recv,
            device_id=where, device_id_type=MESH,
        )

    half = peers // 2
    side, place = lax.rem(me, 2), me // 2
    pair = {"streams": me + 1 - 2 * side}
    small = ((down, downg), (dest, destall), (up, upg))

    def small_copy(i, o):
        src, dst = small[i]
        to = {"streams": 2 * lax.rem(place + o, half) + side}
        return remote(src, dst.at[side, place], g_send.at[i, o], g_recv.at[i, o], to)

    def pair_copy(i):
        dst = small[i][1]
        return remote(dst.at[side], dst.at[side], g_send.at[i, 0], g_recv.at[i, 0], pair)

    def relay(i):
        def arrive(o, c):
            small_copy(i, o).wait()
            return c

        lax.fori_loop(1, half, arrive, 0)
        pair_copy(i).start()

    def cache_copy(o):
        to = lax.rem(me + o, peers)
        return remote(
            outgoing.at[to], arrived.at[me],
            c_send.at[o], c_recv.at[o], {"streams": to},
        )

    def frame_copy(o):
        to = {"mp": lax.rem(my + o, mps)}
        return remote(gathered.at[my], gathered.at[my], f_send.at[o], f_recv.at[o], to)

    def low_copy(o):
        to = {"mp": lax.rem(my + o, mps)}
        return remote(lows.at[my], lows.at[my], l_send.at[o], l_recv.at[o], to)

    downg[side, place] = down[...]
    destall[side, place] = dest[...]
    upg[side, place] = up[...]

    def start_small(o, c):
        for i in range(3):
            small_copy(i, o).start()
        return c

    lax.fori_loop(1, half, start_small, 0)

    def start_rest(o, c):
        q = lax.rem(me + o, peers)
        picks = [jnp.int32(0)] * per_peer
        for s in reversed(range(count)):
            fits = dest_s[s] == q
            picks = [
                jnp.where(fits, new, old) for new, old in zip([jnp.int32(s)] + picks[:-1], picks)
            ]
        for r, p in enumerate(picks):
            one = jnp.concatenate(
                [
                    cache32.at[j][pl.ds(p, hist, stride=count), :]
                    for j in range(width // 128)
                ],
                axis=1,
            )
            outgoing[q, r * length:(r + 1) * length, :] = jnp.concatenate(
                [one, blank], axis=0
            ).astype(BF16)

        @pl.when(o < peers)
        def _():
            cache_copy(o).start()

        return c

    for o in range(1, mps):
        frame_copy(o).start()
    lax.fori_loop(1, peers + 1, start_rest, 0)

    arrived[me] = outgoing[me]

    w_copy.wait()

    def split(i, c):
        at = pl.ds(pl.multiple_of(i * 64, 64), 64)
        both = raw[at].astype(F32)
        weight[at, :width] = both[:, 0, :].astype(BF16)
        weight[at, width:] = both[:, 1, :].astype(BF16)
        return c

    lax.fori_loop(0, mps * width // 64, split, 0)
    for i in range(3):
        relay(i)
    acc[...] = jnp.dot(
        mine, weight[pl.ds(pl.multiple_of(my * width, width), width), :],
        preferred_element_type=F32,
    )

    lane = iota((1, rows), 1) % count
    slot = jnp.zeros((1, rows), jnp.int32)
    for s in range(count):
        slot = jnp.where(lane == s, panel_s[tenant_s[s]], slot)

    for i in range(3):
        pair_copy(i).wait()
    panels = downg[...].reshape(peers * rank_dim, width)
    projected = lax.dot_general(
        panels, mine, (((1,), (1,)), ((), ())), preferred_element_type=F32
    )
    at = iota((peers * rank_dim, rows), 0) // rank_dim
    hit = at == (slot % 2) * half + slot // 2
    part = jnp.where(hit, projected, 0.0).reshape(peers, rank_dim, rows).sum(axis=0)
    lows[my] = part
    for o in range(1, mps):
        low_copy(o).start()

    to_me = (destall[...].reshape(peers, 8, 128)[:, 0, :] == me) & (iota((peers, 128), 1) < count)
    hits = jnp.where(to_me, 1.0, 0.0)
    tri = jnp.where(iota((128, 128), 0) < iota((128, 128), 1), 1.0, 0.0)
    earlier = jnp.dot(hits.astype(BF16), tri.astype(BF16), preferred_element_type=F32)
    at = iota((peers, 128), 0)
    owner = (2 * (at % half) + at // half).astype(F32)
    bucket = jnp.sum(hits * (owner * per_peer + earlier), axis=0, keepdims=True)
    eye = jnp.where(iota((128, 128), 0) == iota((128, 128), 1), 1.0, 0.0)
    column = lax.dot_general(
        eye.astype(BF16), jnp.broadcast_to(bucket, (128, 128)).astype(BF16),
        (((1,), (1,)), ((), ())), preferred_element_type=F32,
    )
    found = column[:count, :].astype(jnp.int32)
    source = found * length
    blocks = peers * chunk
    lanes_all = hist * count
    wanted = jnp.concatenate([source] * (blocks // 128), axis=1)
    wanted = iota((count, blocks), 1) - wanted
    for t in range(hist):
        select[t] = jnp.where(wanted == t, 1.0, 0.0).astype(BF16)

    for o in range(1, mps):
        frame_copy(o).wait()
        j = lax.rem(my + mps - o, mps)
        acc[...] += jnp.dot(
            gathered[j], weight[pl.ds(pl.multiple_of(j * width, width), width), :],
            preferred_element_type=F32,
        )
    for o in range(1, mps):
        low_copy(o).wait()
    low = lows[0]
    for j in range(1, mps):
        low = low + lows[j]
    low = low.astype(BF16).astype(F32)
    spread = jnp.where(
        hit, jnp.broadcast_to(low[None], (peers, rank_dim, rows)).reshape(peers * rank_dim, rows), 0.0
    )
    acc[...] += jnp.dot(
        spread.T.astype(BF16), upg[...].reshape(peers * rank_dim, 2 * width),
        preferred_element_type=F32,
    )

    pre = acc[...]
    gated = (pre[:, :width] * jax.nn.sigmoid(pre[:, width:])).astype(BF16)
    seq[pl.ds(hist, fr)] = gated.astype(F32).reshape(fr, count, width)

    def wait_cache(o, c):
        cache_copy(o).wait()
        return c

    lax.fori_loop(1, peers, wait_cache, 0)
    moved = jnp.dot(
        select[...].reshape(lanes_all, blocks), arrived[...].reshape(blocks, width),
        preferred_element_type=F32,
    )
    seq[pl.ds(0, hist)] = moved.reshape(hist, count, width)

    limit = jnp.zeros((count, 128), jnp.int32)
    sub = iota((count, 128), 0)
    for s in range(count):
        limit = jnp.where(sub == s, valid_s[s] * CH, limit)
    seg = 8
    for sb in range(count // seg):
        keep = limit[sb * seg:(sb + 1) * seg][None] > iota((fr, seg, 128), 0)

        def column_block(cb, c, sb=sb, keep=keep):
            lanes = pl.ds(pl.multiple_of(cb * 128, 128), 128)
            total = jnp.zeros((fr, seg, 128), F32)
            for k in range(hist + 1):
                window = seq[pl.ds(k, fr), pl.ds(sb * seg, seg), lanes]
                total = total + window * taps[pl.ds(k, 1), lanes][None]
            normed = total * scale[lanes].reshape(1, 1, 128) + offset[lanes].reshape(1, 1, 128)
            active = normed * jax.nn.sigmoid(normed)
            enc[:, pl.ds(sb * seg, seg), lanes] = jnp.where(keep, active, 0.0)
            return c

        lax.fori_loop(0, width // 128, column_block, 0)
    back = jnp.where(r_i == (c_i % count) * fr + c_i // count, 1.0, 0.0).astype(BF16)
    out[...] = jnp.dot(
        back, enc[...].reshape(rows, width).astype(BF16), preferred_element_type=F32
    ).astype(BF16)


def local(
    frames, convolution_cache, destination, tenant, valid, tenant_panel_slot, input_weight,
    tenant_down_weight, tenant_up_weight, depthwise_taps, batchnorm_scale, batchnorm_offset,
):
    peers = lax.axis_size("streams")
    mps = lax.axis_size("mp")
    count = destination.shape[0]
    rows, width = frames.shape
    fr = rows // count
    hist = convolution_cache.shape[1]
    length = -(-hist // 16) * 16
    per_peer = max(1, count // peers)
    rank_dim = tenant_down_weight.shape[2]
    smem = pl.BlockSpec(memory_space=pltpu.SMEM)
    vmem = pl.BlockSpec(memory_space=pltpu.VMEM)
    dims = (peers, mps, count, fr, hist, length, width, per_peer, rank_dim)
    dma = pltpu.SemaphoreType.DMA
    return pl.pallas_call(
        functools.partial(kernel, dims),
        out_shape=jax.ShapeDtypeStruct((rows, width), BF16),
        in_specs=[smem] * 4 + [vmem] * 2 + [pl.BlockSpec(memory_space=pl.ANY)] + [vmem] * 5,
        out_specs=vmem,
        scratch_shapes=[
            pltpu.VMEM((mps, rows, width), BF16),
            pltpu.VMEM((peers, length * per_peer, width), BF16),
            pltpu.VMEM((peers, length * per_peer, width), BF16),
            pltpu.VMEM((8, 128), jnp.int32),
            pltpu.VMEM((2, peers // 2, 8, 128), jnp.int32),
            pltpu.VMEM((hist, count, peers * length * per_peer), BF16),
            pltpu.VMEM((2, peers // 2, rank_dim, width), BF16),
            pltpu.VMEM((2, peers // 2, rank_dim, 2 * width), BF16),
            pltpu.VMEM((mps, rank_dim, rows), F32),
            pltpu.VMEM((rank_dim, 2 * width), BF16),
            pltpu.VMEM((width // 128, hist * count, 128), F32),
            pltpu.VMEM((mps * width, 2, width), BF16),
            pltpu.VMEM((mps * width, 2 * width), BF16),
            pltpu.VMEM((rows, 2 * width), F32),
            pltpu.VMEM((hist + fr, count, width), F32),
            pltpu.VMEM((fr, count, width), F32),
            dma,
            dma((mps,)), dma((mps,)),
            dma((peers,)), dma((peers,)),
            dma((3, peers // 2)), dma((3, peers // 2)),
            dma((mps,)), dma((mps,)),
        ],
        compiler_params=pltpu.CompilerParams(
            collective_id=0, has_side_effects=True, vmem_limit_bytes=56 * 1024 * 1024
        ),
    )(
        destination, tenant, valid, tenant_panel_slot,
        frames, convolution_cache.transpose(1, 0, 2),
        input_weight,
        tenant_down_weight[0].T, tenant_up_weight[0],
        depthwise_taps, batchnorm_scale, batchnorm_offset,
    )


def solution(mesh):
    in_specs = (
        P("streams", "mp"),
        P("streams", None, "mp"),
        P("streams"),
        P("streams"),
        P("streams"),
        P(),
        P(None, None, "mp"),
        P("streams", "mp", None),
        P("streams", None, None, "mp"),
        P(None, "mp"),
        P("mp"),
        P("mp"),
    )
    return jax.shard_map(
        local, mesh=mesh, in_specs=in_specs, out_specs=P("streams", "mp"), check_vma=False
    )
```
